32 devices in a mesh: ctx: 8 (over z, y), grp: 2 (over core), head: 2 (over x).
Axes of the slice: x: 2, y: 2, z: 4, core: 2. Of those that a mesh axis runs over, the one named last changes fastest.
Arguments:
- residual: bfloat16 [2048, 2880], P(('ctx', 'grp')), may hold values from -10 to 10
- queries: bfloat16 [2048, 2048], P(('ctx', 'grp'), 'head'), may hold values from -32 to 32
- keys: bfloat16 [2048, 256], P(('ctx', 'grp'), 'head'), may hold values from -32 to 32
- values: bfloat16 [2048, 256], P(('ctx', 'grp'), 'head'), may hold values from -12 to 12
- out_weight: bfloat16 [2048, 2880], P('head'), may hold values from -0.125 to 0.125
- norm_gain: float32 [2880], replicated, may hold values from 0.5 to 1.5
- routes: int32 [2048, 4], P(('ctx', 'grp')), may hold values from 0 to 7, all different within a row; in each aligned block of 128 rows (0 to 127, 128 to 255, ...) at most 72 rows name the same one
- expert_weight: bfloat16 [8, 2880, 2, 1536], P('ctx', None, None, 'head'), may hold values from -0.109375 to 0.109375
Outputs:
- hidden: bfloat16 [2048, 2880], P(('ctx', 'grp'), 'head')
- active: bfloat16 [8, 2, 576, 1536], P('ctx', 'grp', None, 'head')
The draws below stay inside these ranges and needn't reach their ends.
Inputs may be any that keep to these rules, and one draw needn't show every extreme that they name: `routes`: each token names 4 different experts; the 128 rows of one device name any one expert at most 72 times.
All inputs are finite; a program needn't handle non-finite values.
Results may differ from the reference program's by a relative error of at most 0.017.
Values may be sent and summed in bfloat16 or wider, within the bound.
A program may use at most 128 MiB of HBM per device.

```python
import math
import jax
import jax.numpy as jnp
import numpy as np
from jax import lax

D = 2880
HD = 64
HEADS = 32
KV_HEADS = 4
FFW = 1536
TOP = 4
TOK_DEV = 128
EXPERTS = 8
CAP = 72
CYCLE = 1
WINDOW = 256
TOKENS = 2048
N_CTX = 8
N_GRP = 2
N_HEAD = 2


def draw_queries(key, part):
    drawn_key = jax.random.fold_in(key, 1)
    drawn = jnp.clip(jax.random.normal(drawn_key, (TOKENS, HEADS * HD)), -4.0, 4.0)
    return drawn.astype(jnp.bfloat16)


def draw_keys(key, part):
    drawn_key = jax.random.fold_in(key, 2)
    drawn = jnp.clip(jax.random.normal(drawn_key, (TOKENS, KV_HEADS * HD)), -4.0, 4.0)
    return drawn.astype(jnp.bfloat16)


def draw_residual(key, part):
    row_key, value_key, column_key = jax.random.split(jax.random.fold_in(key, 3), 3)
    row_scale = jnp.exp(jax.random.uniform(row_key, (TOKENS, 1), minval=jnp.log(0.1), maxval=0.0))
    places = jnp.arange(D, dtype=jnp.float32) / (D - 1)
    jitter = jnp.exp(jax.random.uniform(column_key, (1, D), minval=jnp.log(0.7), maxval=jnp.log(1.4)))
    column_scale = jnp.exp(places * jnp.log(3.0))[None, :] / 1.7 * jitter
    entries = jnp.clip(jax.random.normal(value_key, (TOKENS, D)), -4.0, 4.0)
    return (entries * row_scale * column_scale).astype(jnp.bfloat16)


def steps_of(key, dims, pieces, low, largest):
    factor_of = 1.0
    for position, shards_of in pieces:
        heights = jax.random.uniform(jax.random.fold_in(jax.random.fold_in(key, 6), position), (shards_of,), jnp.float32, low / len(pieces), largest / len(pieces))
        factor_of = factor_of * jnp.repeat(jnp.exp(heights), dims[position] // shards_of).reshape((-1,) + (1,) * (len(dims) - 1 - position))
    return factor_of


def shared_out(rng, own, number, rows, count, top, reach, slope):
    order = jax.random.permutation(rng, count)
    packed, usual = shares(count, rows * top, reach, slope, True), shares(count, rows * top, reach, slope, False)
    places = jnp.arange(count)

    def named(lengths, turn):
        used = int((lengths > 0).sum())
        fixed = max(1, used // 4)
        passed = fixed + (places - fixed + turn * (used - fixed)) % max(1, count - fixed)
        return jnp.zeros((count,), jnp.int32).at[order[jnp.where(places < fixed, places, passed)]].set(jnp.asarray(lengths, jnp.int32))

    lengths = jnp.where(number % 4 == 0, named(packed, number // 4), named(usual, number - number // 4 - 1))
    mixed = jax.random.permutation(jax.random.fold_in(own, 3), count)
    giver, sink = mixed[0:count // 2 * 2:2], mixed[1:count // 2 * 2:2]
    margin = jnp.minimum(lengths[giver] - 1, reach - lengths[sink]) // 2
    margin = jnp.where((giver == order[0]) | (sink == order[0]) | (lengths[sink] == 0), 0, jnp.maximum(margin, 0))
    passed = jax.random.randint(jax.random.fold_in(own, 4), (count // 2,), 0, 1 << 20) % (margin + 1)
    lengths = lengths.at[giver].add(-passed).at[sink].add(passed)
    members = jnp.searchsorted(jnp.cumsum(lengths), jnp.arange(rows * top), side="right").astype(jnp.int32)
    table = members.reshape(top, rows).T
    table = table[jax.random.permutation(jax.random.fold_in(own, 1), rows)]
    turn = jax.random.randint(jax.random.fold_in(own, 2), (rows, 1), 0, top)
    return jnp.take_along_axis(table, (jnp.arange(top)[None, :] + turn) % top, axis=1)


def shares(number_of, total, bound, skew, full):
    portions = [(1 << 20) // math.isqrt(grade ** skew) + 1 for grade in range(1, number_of + 1)]
    largest = bound if full else min(bound, max(-(-total // number_of), total * portions[0] // sum(portions)))
    least = 1 if total - largest >= number_of - 1 else 0
    counts, surplus = [largest] + [least] * (number_of - 1), total - largest - least * (number_of - 1)
    while surplus > 0:
        candidates = [i for i in range(1, number_of) if counts[i] < largest] or [i for i in range(1, number_of) if counts[i] < bound]
        pool, remaining = sum([portions[i] for i in candidates]), surplus
        for i in candidates:
            extra = min(bound - counts[i], max(1, remaining * portions[i] // pool), surplus)
            counts[i] = counts[i] + extra
            surplus = surplus - extra
    return np.array(counts)


def gaussian(rng, shape, width, most, shards=(), kind=jnp.bfloat16):
    drawn = width * jax.random.normal(rng, shape, jnp.float32)
    if shards:
        drawn = drawn * steps_of(rng, shape, shards, -0.22, 0.18)
    return jnp.clip(drawn, -most, most).astype(kind)


def setup_inputs(seed: int = 0) -> dict:
    key_list = jax.random.split(jax.random.key(seed), 9)
    residual = draw_residual(jax.random.fold_in(key_list[8], 71), 0)
    queries = draw_queries(jax.random.fold_in(key_list[8], 71), 0)
    keys = draw_keys(jax.random.fold_in(key_list[8], 71), 0)
    values = gaussian(key_list[3], (TOKENS, KV_HEADS * HD), 2.0, 12.0, ((0, 16), (1, 2)))
    out_weight = gaussian(key_list[4], (HEADS * HD, D), (HEADS * HD) ** -0.5, 0.125, ((0, 2),))
    norm_gain = jnp.clip(1.0 + 0.1 * jax.random.normal(key_list[5], (D,), jnp.float32), 0.5, 1.5)
    routes_keys = jax.random.split(jax.random.fold_in(key_list[6], 1), TOKENS // TOK_DEV)
    routes_turns = jax.random.permutation(jax.random.fold_in(key_list[6], 3), TOKENS // TOK_DEV)
    routes = jax.vmap(lambda own, number: shared_out(jax.random.fold_in(key_list[6], 2), own, number, TOK_DEV, EXPERTS, TOP, CAP, 1))(routes_keys, routes_turns).reshape((TOKENS, TOP))
    expert_weight = gaussian(key_list[7], (EXPERTS, D, 2, FFW), D ** -0.5, 0.109375, ((0, 8), (3, 2)))
    return dict(residual=residual, queries=queries, keys=keys, values=values, out_weight=out_weight, norm_gain=norm_gain, routes=routes, expert_weight=expert_weight)


def attend_rows(query_block, key_window, value_window, query_place, key_place):
    scores = jnp.einsum('bgd,wd->gbw', query_block.astype(jnp.float32), key_window.astype(jnp.float32)) * HD ** (-0.5)
    allowed = (key_place[None, :] <= query_place[:, None]) & (query_place[:, None] - key_place[None, :] < WINDOW) & (key_place[None, :] >= 0)
    scores = jnp.where(allowed[None], scores, -1e+30)
    row_max = lax.optimization_barrier(jnp.max(scores, axis=-1, keepdims=True))
    weights = jnp.where(allowed[None], jnp.exp(scores - row_max), 0.0)
    row_total = lax.optimization_barrier(jnp.sum(weights, axis=-1))
    rounded = lax.optimization_barrier(weights.astype(jnp.bfloat16))
    mixed = jnp.einsum('gbw,wd->gbd', rounded.astype(jnp.float32), value_window.astype(jnp.float32))
    return mixed / row_total[..., None]

def reference(residual, queries, keys, values, out_weight, norm_gain, routes, expert_weight):
    per_group = HEADS // KV_HEADS
    block_len = TOK_DEV * N_GRP
    reach_len = CYCLE * block_len
    pad_keys = jnp.concatenate([jnp.zeros((reach_len, KV_HEADS * HD), keys.dtype), keys], 0)
    pad_values = jnp.concatenate([jnp.zeros((reach_len, KV_HEADS * HD), values.dtype), values], 0)

    def one_block(block_index):
        first_row = (block_index * block_len).astype(jnp.int32)
        query_block = lax.dynamic_slice_in_dim(queries, first_row, block_len, 0).reshape(block_len, KV_HEADS, per_group, HD)
        key_window = lax.dynamic_slice_in_dim(pad_keys, first_row, reach_len + block_len, 0).reshape(reach_len + block_len, KV_HEADS, HD)
        value_window = lax.dynamic_slice_in_dim(pad_values, first_row, reach_len + block_len, 0).reshape(reach_len + block_len, KV_HEADS, HD)
        query_place = first_row + jnp.arange(block_len, dtype=jnp.int32)
        key_place = first_row - reach_len + jnp.arange(reach_len + block_len, dtype=jnp.int32)

        def one_head(operands):
            head_queries, head_keys, head_values = operands
            return attend_rows(head_queries, head_keys, head_values, query_place, key_place)
        heads_out = lax.map(one_head, (jnp.moveaxis(query_block, 1, 0), jnp.moveaxis(key_window, 1, 0), jnp.moveaxis(value_window, 1, 0)))
        return jnp.transpose(heads_out, (2, 0, 1, 3)).reshape(block_len, HEADS * HD).astype(jnp.bfloat16)
    attended = lax.map(one_block, jnp.arange(N_CTX, dtype=jnp.int32)).reshape(TOKENS, HEADS * HD)
    slice_len = HEADS * HD // N_HEAD
    projected = jnp.zeros((TOKENS, D), jnp.float32)
    for head_part in range(N_HEAD):
        partial_value = jnp.dot(attended[:, head_part * slice_len:(head_part + 1) * slice_len], out_weight[head_part * slice_len:(head_part + 1) * slice_len], preferred_element_type=jnp.float32)
        projected = projected + lax.optimization_barrier(partial_value.astype(jnp.bfloat16)).astype(jnp.float32)
    hidden = (residual.astype(jnp.float32) + projected).astype(jnp.bfloat16)
    devices_all = TOKENS // TOK_DEV
    per_device = routes.astype(jnp.int32).reshape(devices_all, TOK_DEV * TOP)
    expert_ids = jnp.arange(EXPERTS, dtype=jnp.int32)

    def ranks_of(device_routes):
        expert_hits = (device_routes[:, None] == expert_ids[None, :]).astype(jnp.int32)
        before = (jnp.cumsum(expert_hits, axis=0) - expert_hits).astype(jnp.int32)
        return lax.optimization_barrier(jnp.sum(before * expert_hits, axis=1)).astype(jnp.int32)
    slot_index = lax.map(ranks_of, per_device).reshape(TOKENS, TOP).astype(jnp.int32)
    token_ids = jnp.arange(TOKENS, dtype=jnp.int32)
    source = token_ids // TOK_DEV
    source_grp = (source % N_GRP).astype(jnp.int32)
    source_ctx = (source // N_GRP).astype(jnp.int32)
    row_index = (source_ctx[:, None] * CAP + slot_index).astype(jnp.int32)
    slot_table = jnp.full((EXPERTS, N_GRP, N_CTX * CAP), TOKENS, jnp.int32)
    slot_table = slot_table.at[routes.astype(jnp.int32), jnp.broadcast_to(source_grp[:, None], (TOKENS, TOP)), row_index].set(jnp.broadcast_to(token_ids[:, None], (TOKENS, TOP)))
    padded = jnp.concatenate([hidden, jnp.zeros((1, D), hidden.dtype)], 0)

    def expert_rows(operands):
        expert_table, weight = operands
        route_rows = padded[expert_table.reshape(-1)].astype(jnp.float32)
        squares = lax.optimization_barrier(jnp.sum(route_rows * route_rows, axis=1))
        scaled = (route_rows * norm_gain[None, :]).astype(jnp.bfloat16)
        gate_up = jnp.dot(scaled, weight.reshape(D, 2 * FFW), preferred_element_type=jnp.float32)
        inverse_rms = lax.rsqrt(squares / D + 1e-05)
        gate_part = gate_up[:, :FFW] * inverse_rms[:, None]
        up_part = gate_up[:, FFW:] * inverse_rms[:, None]
        result = (gate_part * jax.nn.sigmoid(1.702 * gate_part) * (up_part + 1.0)).astype(jnp.bfloat16)
        return result.reshape(N_GRP, N_CTX * CAP, FFW)
    active = lax.map(expert_rows, (slot_table, expert_weight))
    return (hidden, active)
```

```python
import functools
import jax
import jax.numpy as jnp
from jax import lax
from jax.experimental import pallas as pl
from jax.experimental.pallas import tpu as pltpu
from jax.sharding import PartitionSpec as P

D = 2880
HD = 64
TOP = 4


def shifted(value, axis, by):
    count = lax.axis_size(axis)
    pairs = [(i, i + by) for i in range(count) if 0 <= i + by < count]
    return lax.ppermute(value, axis, pairs)


def attend_block(running, query_heads, key_block, value_block, query_place, key_place, band):
    allowed = (
        (key_place[None, :] <= query_place[:, None])
        & (query_place[:, None] - key_place[None, :] < band)
        & (key_place[None, :] >= 0)
    )

    def attend_live(carried):
        row_max, row_total, summed = carried
        scores = jnp.einsum(
            "tkgd,skd->kgts", query_heads, key_block, preferred_element_type=jnp.float32
        )
        scores = jnp.where(allowed, scores * query_heads.shape[-1] ** (-0.5), -1e30)
        new_max = jnp.maximum(row_max, jnp.max(scores, axis=-1))
        weights = jnp.where(allowed, jnp.exp(scores - new_max[..., None]), 0.0)
        factor = jnp.exp(row_max - new_max)
        row_total = row_total * factor + jnp.sum(weights, axis=-1)
        summed = summed * factor[..., None] + jnp.einsum(
            "kgts,skd->kgtd",
            weights.astype(jnp.bfloat16),
            value_block,
            preferred_element_type=jnp.float32,
        )
        return (new_max, row_total, summed)

    def skip_block(carried):
        return carried

    return lax.cond(jnp.any(allowed), attend_live, skip_block, running)


MESH = pl.DeviceIdType.MESH
F32 = jnp.float32
BF16 = jnp.bfloat16


def turn_of(step, count):
    return 1 + lax.rem(step + count // 2 - 1, count - 1)


def layer_kernel(
    count,
    cap,
    att_ref,
    res_ref,
    routes_ref,
    gain_ref,
    ow_hbm,
    w_hbm,
    hid_ref,
    act_ref,
    ow,
    w,
    psend,
    precv,
    hits_ref,
    before_ref,
    sbuf,
    rbuf,
    ow_sem,
    w_sem,
    psend_sem,
    precv_sem,
    send_sem,
    recv_sem,
    xsend_sem,
    xrecv_sem,
):
    me = lax.axis_index("ctx")
    head = lax.axis_index("head")
    heads = rbuf.shape[0]
    others = [lax.rem(head + j, heads) for j in range(1, heads)]
    half, tokens = hid_ref.shape
    width = act_ref.shape[2]

    def ow_copy(which, slot):
        rows = pl.ds(pl.multiple_of(which * half, 16), half)
        return pltpu.make_async_copy(ow_hbm.at[rows], ow.at[slot], ow_sem.at[slot])

    for j in range(1, heads):
        ow_copy(others[j - 1], j).start()
    ow_copy(head, 0).start()
    pltpu.make_async_copy(w_hbm, w, w_sem).start()

    barrier = pltpu.get_barrier_semaphore()
    for other in others:
        pl.semaphore_signal(barrier, inc=1, device_id={"head": other}, device_id_type=MESH)

    def greet(step, carry):
        peer = lax.rem(me + step, count)
        pl.semaphore_signal(barrier, inc=1, device_id={"ctx": peer}, device_id_type=MESH)
        return carry

    lax.fori_loop(1, count, greet, 0)

    def project(slot):
        return lax.dot_general(
            ow[slot], att_ref[...], (((1,), (1,)), ((), ())), preferred_element_type=F32
        ).astype(BF16)

    def exchange(j):
        return pltpu.make_async_remote_copy(
            src_ref=psend.at[j - 1],
            dst_ref=precv.at[j - 1],
            send_sem=psend_sem.at[j - 1],
            recv_sem=precv_sem.at[j - 1],
            device_id={"head": others[j - 1]},
            device_id_type=MESH,
        )

    for j in range(1, heads):
        ow_copy(others[j - 1], j).wait()
        psend[j - 1] = project(j)
        if j == 1:
            pl.semaphore_wait(barrier, count - 1 + heads - 1)
        exchange(j).start()
    ow_copy(head, 0).wait()
    projected = project(0).astype(F32)

    expert_ids = lax.broadcasted_iota(jnp.int32, (count, tokens), 0)
    hits = jnp.zeros((count, tokens), F32)
    for k in range(routes_ref.shape[0]):
        hits = hits + jnp.where(routes_ref[k : k + 1, :] == expert_ids, 1.0, 0.0)
    earlier = jnp.where(
        lax.broadcasted_iota(jnp.int32, (tokens, tokens), 0)
        < lax.broadcasted_iota(jnp.int32, (tokens, tokens), 1),
        1.0,
        0.0,
    ).astype(BF16)
    hits_ref[...] = hits
    before_ref[...] = jnp.dot(hits.astype(BF16), earlier, preferred_element_type=F32)
    residual = res_ref[pl.ds(pl.multiple_of(head * half, 16), half), :].astype(F32)

    for j in range(1, heads):
        exchange(j).wait()
        projected = projected + precv[j - 1].astype(F32)
    hid_ref[...] = (residual + projected).astype(BF16)

    slots = lax.broadcasted_iota(jnp.int32, (cap, tokens), 0).astype(F32)

    def rows_for(expert):
        wanted = hits_ref[pl.ds(expert, 1), :] > 0.5
        picks = jnp.where((slots == before_ref[pl.ds(expert, 1), :]) & wanted, 1.0, 0.0)
        return lax.dot_general(
            picks.astype(BF16),
            hid_ref[...],
            (((1,), (1,)), ((), ())),
            preferred_element_type=F32,
        ).astype(BF16)

    def routed(step):
        turn = turn_of(step, count)
        return pltpu.make_async_remote_copy(
            src_ref=sbuf.at[turn],
            dst_ref=rbuf.at[head, me],
            send_sem=send_sem.at[turn],
            recv_sem=recv_sem.at[me],
            device_id={"ctx": lax.rem(me + turn, count)},
            device_id_type=MESH,
        )

    def landed(source):
        return pltpu.make_async_remote_copy(
            src_ref=rbuf.at[head, source],
            dst_ref=rbuf.at[head, source],
            send_sem=send_sem.at[0],
            recv_sem=recv_sem.at[source],
            device_id={"head": others[0]},
            device_id_type=MESH,
        )

    def crossed(j, source):
        return pltpu.make_async_remote_copy(
            src_ref=rbuf.at[head, source],
            dst_ref=rbuf.at[head, source],
            send_sem=xsend_sem.at[j - 1, source],
            recv_sem=xrecv_sem.at[j - 1, source],
            device_id={"head": others[j - 1]},
            device_id_type=MESH,
        )

    def cross(source):
        for j in range(1, heads):
            crossed(j, source).start()

    def mirror(source):
        for j in range(1, heads):
            origin = lax.rem(head + heads - j, heads)
            pltpu.make_async_remote_copy(
                src_ref=rbuf.at[origin, source],
                dst_ref=rbuf.at[origin, source],
                send_sem=xsend_sem.at[j - 1, source],
                recv_sem=xrecv_sem.at[j - 1, source],
                device_id={"head": others[j - 1]},
                device_id_type=MESH,
            ).wait_recv()

    def dispatch(step, carry):
        turn = turn_of(step, count)
        sbuf[turn] = rows_for(lax.rem(me + turn, count))
        routed(step).start()
        return carry

    lax.fori_loop(0, count - 1, dispatch, 0)
    rbuf[head, me] = rows_for(me)
    cross(me)
    pltpu.make_async_copy(w_hbm, w, w_sem).wait()

    def expert(source):
        squares = jnp.zeros((cap, 1), F32)
        parts = []
        for part in range(heads):
            rows = rbuf[part, source].astype(F32)
            squares = squares + jnp.sum(rows * rows, axis=1, keepdims=True)
            parts.append((rows * gain_ref[part : part + 1, :]).astype(BF16))
        inverse_rms = lax.rsqrt(squares / (heads * half) + 1e-05)

        def product(low):
            total = jnp.zeros((cap, width), F32)
            for part in range(heads):
                total = total + jnp.dot(
                    parts[part],
                    w[part * half : (part + 1) * half, low : low + width],
                    preferred_element_type=F32,
                )
            return total

        gate = product(0) * inverse_rms
        up = product(width) * inverse_rms
        act_ref[source] = (gate * jax.nn.sigmoid(1.702 * gate) * (up + 1.0)).astype(BF16)

    def receive(step, carry):
        source = lax.rem(me + count - turn_of(step, count), count)
        landed(source).wait_recv()
        cross(source)
        before = jnp.where(
            step == 0, me, lax.rem(me + count - turn_of(jnp.maximum(step - 1, 0), count), count)
        )
        mirror(before)
        expert(before)
        return carry

    lax.fori_loop(0, count - 1, receive, 0)
    last = lax.rem(me + count - turn_of(count - 2, count), count)
    mirror(last)
    expert(last)

    def drain(step, carry):
        routed(step).wait_send()
        for j in range(1, heads):
            crossed(j, lax.rem(me + step + 1, count)).wait_send()
        return carry

    lax.fori_loop(0, count - 1, drain, 0)
    for j in range(1, heads):
        crossed(j, me).wait_send()


def body(residual, queries, keys, values, out_weight, norm_gain, routes, expert_weight):
    tokens_here = queries.shape[0]
    kv_local = keys.shape[1] // HD
    per_group = queries.shape[1] // keys.shape[1]
    query_heads = queries.reshape(tokens_here, kv_local, per_group, HD)
    ctx_index = lax.axis_index("ctx")
    grp_index = lax.axis_index("grp")
    head_index = lax.axis_index("head")
    heads_count = lax.axis_size("head")
    block_len = tokens_here * lax.axis_size("grp")
    reach_steps = max(1, lax.axis_size("ctx") // 16)
    band = reach_steps * block_len
    query_place = (
        ctx_index * block_len + grp_index * tokens_here + jnp.arange(tokens_here, dtype=jnp.int32)
    )
    own_keys, own_values = (
        lax.all_gather(keys, "grp", axis=0, tiled=True),
        lax.all_gather(values, "grp", axis=0, tiled=True),
    )

    def attend_from(running, key_flat, value_flat, distance):
        key_place = (ctx_index - distance) * block_len + jnp.arange(block_len, dtype=jnp.int32)
        return attend_block(
            running,
            query_heads,
            key_flat.reshape(block_len, kv_local, HD),
            value_flat.reshape(block_len, kv_local, HD),
            query_place,
            key_place,
            band,
        )

    running = (
        jnp.full((kv_local, per_group, tokens_here), -1e30, jnp.float32),
        jnp.zeros((kv_local, per_group, tokens_here), jnp.float32),
        jnp.zeros((kv_local, per_group, tokens_here, HD), jnp.float32),
    )
    running = attend_from(running, own_keys, own_values, 0)

    def cycle_turn(distance, carried):
        running, key_flat, value_flat = carried
        key_flat, value_flat = shifted((key_flat, value_flat), "ctx", 1)
        running = attend_from(running, key_flat, value_flat, distance)
        return (running, key_flat, value_flat)

    running = lax.fori_loop(1, reach_steps + 1, cycle_turn, (running, own_keys, own_values))[0]
    row_max, row_total, summed = running
    mixed = summed / row_total[..., None]
    attended = (
        jnp.transpose(mixed, (2, 0, 1, 3))
        .reshape(tokens_here, kv_local * per_group * HD)
        .astype(jnp.bfloat16)
    )
    width_all = residual.shape[1]
    half = width_all // heads_count
    count = lax.axis_size("ctx")
    experts_all = expert_weight.shape[0] * count
    routed = tokens_here * TOP
    cap = min(tokens_here, routed // experts_all + max(1, routed // (8 * experts_all)))
    hidden_width = expert_weight.shape[3]
    in_vmem = pl.BlockSpec(memory_space=pltpu.VMEM)
    in_hbm = pl.BlockSpec(memory_space=pl.ANY)
    hidden, active = pl.pallas_call(
        functools.partial(layer_kernel, count, cap),
        out_shape=(
            jax.ShapeDtypeStruct((half, tokens_here), BF16),
            jax.ShapeDtypeStruct((count, cap, hidden_width), BF16),
        ),
        in_specs=[in_vmem] * 4 + [in_hbm] * 2,
        out_specs=(in_vmem, in_vmem),
        scratch_shapes=[
            pltpu.VMEM((heads_count, half, out_weight.shape[0]), BF16),
            pltpu.VMEM((width_all, 2 * hidden_width), BF16),
            pltpu.VMEM((heads_count - 1, half, tokens_here), BF16),
            pltpu.VMEM((heads_count - 1, half, tokens_here), BF16),
            pltpu.VMEM((count, tokens_here), F32),
            pltpu.VMEM((count, tokens_here), F32),
            pltpu.VMEM((count, cap, half), BF16),
            pltpu.VMEM((heads_count, count, cap, half), BF16),
            pltpu.SemaphoreType.DMA((heads_count,)),
            pltpu.SemaphoreType.DMA,
            pltpu.SemaphoreType.DMA((heads_count - 1,)),
            pltpu.SemaphoreType.DMA((heads_count - 1,)),
            pltpu.SemaphoreType.DMA((count,)),
            pltpu.SemaphoreType.DMA((count,)),
            pltpu.SemaphoreType.DMA((heads_count - 1, count)),
            pltpu.SemaphoreType.DMA((heads_count - 1, count)),
        ],
        compiler_params=pltpu.CompilerParams(
            collective_id=0, has_side_effects=True, vmem_limit_bytes=60 * 1024 * 1024
        ),
    )(
        attended,
        residual.T,
        routes.T,
        norm_gain.reshape(heads_count, half),
        out_weight.T,
        expert_weight[0].reshape(width_all, 2 * hidden_width),
    )
    return (hidden.T, active.reshape(1, 1, count * cap, hidden_width))


def solution(mesh):
    in_specs = (
        P(("ctx", "grp"), None),
        P(("ctx", "grp"), "head"),
        P(("ctx", "grp"), "head"),
        P(("ctx", "grp"), "head"),
        P("head", None),
        P(),
        P(("ctx", "grp"), None),
        P("ctx", None, None, "head"),
    )
    out_specs = (P(("ctx", "grp"), "head"), P("ctx", "grp", None, "head"))
    return jax.shard_map(body, mesh=mesh, in_specs=in_specs, out_specs=out_specs, check_vma=False)
```

```python
import functools
import jax
import jax.numpy as jnp
from jax import lax
from jax.experimental import pallas as pl
from jax.experimental.pallas import tpu as pltpu
from jax.sharding import PartitionSpec as P

D = 2880
HD = 64
TOP = 4


MESH = pl.DeviceIdType.MESH
F32 = jnp.float32
BF16 = jnp.bfloat16


def turn_of(step, count):
    return 1 + lax.rem(step + count // 2 - 1, count - 1)


def in_pair(values, group, lanes):
    zeros = jnp.zeros((values.shape[0], HD), values.dtype)
    if values.shape[1] == HD:
        return jnp.concatenate([values, zeros], 1), jnp.concatenate([zeros, values], 1)
    first = group % 2 == 0
    base = group // 2 * 2 * HD
    pair = values[:, base : base + 2 * HD]
    swapped = jnp.concatenate([pair[:, HD:], pair[:, :HD]], 1)
    low = jnp.where(lanes < HD, pair if first else swapped, jnp.zeros_like(pair))
    high = jnp.where(lanes >= HD, swapped if first else pair, jnp.zeros_like(pair))
    return low, high


def attend(block, reach, q_ref, kbuf, vbuf, att_ref):
    tokens = q_ref.shape[0]
    window = kbuf.shape[0]
    kv_local = kbuf.shape[1] // HD
    pairs = q_ref.shape[1] // (2 * HD * kv_local)
    rows = pairs * tokens
    place = lax.rem(lax.broadcasted_iota(jnp.int32, (rows, window), 0), tokens)
    column = lax.broadcasted_iota(jnp.int32, (rows, window), 1)
    ahead = place + reach * tokens - column
    allowed = (ahead >= 0) & (ahead < reach * tokens) & (column >= (reach - block) * tokens)
    lanes = lax.broadcasted_iota(jnp.int32, (window, 2 * HD), 1)
    left = lax.broadcasted_iota(jnp.int32, (rows, 2 * HD), 1) < HD
    for group in range(kv_local):
        key_pair = in_pair(kbuf[...], group, lanes)
        value_pair = in_pair(vbuf[...], group, lanes)
        first = group * pairs
        queries = jnp.concatenate(
            [
                q_ref[:, (first + p) * 2 * HD : (first + p + 1) * 2 * HD]
                for p in range(pairs)
            ],
            0,
        )
        mixed = jnp.zeros((rows, 2 * HD), F32)
        totals = []
        for side in range(2):
            scores = lax.dot_general(
                queries,
                key_pair[side],
                (((1,), (1,)), ((), ())),
                preferred_element_type=F32,
            )
            scores = jnp.where(allowed, scores * HD ** (-0.5), -1e30)
            row_max = jnp.max(scores, axis=1, keepdims=True)
            weights = jnp.where(allowed, jnp.exp(scores - row_max), 0.0)
            totals.append(jnp.sum(weights, axis=1, keepdims=True))
            mixed = mixed + jnp.dot(
                weights.astype(BF16), value_pair[side], preferred_element_type=F32
            )
        attended = (mixed / jnp.where(left, totals[0], totals[1])).astype(BF16)
        for p in range(pairs):
            att_ref[:, (first + p) * 2 * HD : (first + p + 1) * 2 * HD] = attended[
                p * tokens : (p + 1) * tokens
            ]


def layer_kernel(
    count,
    cap,
    reach,
    q_ref,
    k_ref,
    v_ref,
    res_ref,
    routes_ref,
    gain_ref,
    ow_hbm,
    w_hbm,
    hid_ref,
    act_ref,
    kbuf,
    vbuf,
    att_ref,
    ow,
    w,
    psend,
    precv,
    hits_ref,
    before_ref,
    sbuf,
    rbuf,
    ksend_sem,
    krecv_sem,
    ow_sem,
    w_sem,
    psend_sem,
    precv_sem,
    send_sem,
    recv_sem,
    xsend_sem,
    xrecv_sem,
):
    me = lax.axis_index("ctx")
    head = lax.axis_index("head")
    heads = rbuf.shape[0]
    others = [lax.rem(head + j, heads) for j in range(1, heads)]
    half, tokens = hid_ref.shape
    width = act_ref.shape[2]

    def ow_copy(which, slot):
        rows = pl.ds(pl.multiple_of(which * half, 16), half)
        return pltpu.make_async_copy(ow_hbm.at[rows], ow.at[slot], ow_sem.at[slot])

    for j in range(1, heads):
        ow_copy(others[j - 1], j).start()
    ow_copy(head, 0).start()
    pltpu.make_async_copy(w_hbm, w, w_sem).start()

    barrier = pltpu.get_barrier_semaphore()
    for other in others:
        pl.semaphore_signal(barrier, inc=1, device_id={"head": other}, device_id_type=MESH)

    def greet(step, carry):
        peer = lax.rem(me + step, count)
        pl.semaphore_signal(barrier, inc=1, device_id={"ctx": peer}, device_id_type=MESH)
        return carry

    lax.fori_loop(1, count, greet, 0)

    groups = lax.axis_size("grp")
    block = me * groups + lax.axis_index("grp")
    blocks = count * groups

    def at_block(index):
        return {"ctx": index // groups, "grp": lax.rem(index, groups)}

    for j in range(1, reach + 1):
        for peer in (lax.rem(block + j, blocks), lax.rem(block + blocks - j, blocks)):
            pl.semaphore_signal(barrier, inc=1, device_id=at_block(peer), device_id_type=MESH)

    def window_copies(j):
        place = pl.ds((reach - j) * tokens, tokens)
        target = at_block(lax.rem(block + j, blocks))
        return [
            pltpu.make_async_remote_copy(
                src_ref=source,
                dst_ref=buffer.at[place],
                send_sem=ksend_sem.at[n, j - 1],
                recv_sem=krecv_sem.at[n, j - 1],
                device_id=target,
                device_id_type=MESH,
            )
            for n, (source, buffer) in enumerate(((k_ref, kbuf), (v_ref, vbuf)))
        ]

    pl.semaphore_wait(barrier, count - 1 + heads - 1 + 2 * reach)
    for j in range(1, reach + 1):

        @pl.when(block + j < blocks)
        def _(j=j):
            for copy in window_copies(j):
                copy.start()

    kbuf[reach * tokens :, :] = k_ref[...]
    vbuf[reach * tokens :, :] = v_ref[...]

    def project(slot):
        return lax.dot_general(
            ow[slot], att_ref[...], (((1,), (1,)), ((), ())), preferred_element_type=F32
        ).astype(BF16)

    def exchange(j):
        return pltpu.make_async_remote_copy(
            src_ref=psend.at[j - 1],
            dst_ref=precv.at[j - 1],
            send_sem=psend_sem.at[j - 1],
            recv_sem=precv_sem.at[j - 1],
            device_id={"head": others[j - 1]},
            device_id_type=MESH,
        )

    for j in range(1, reach + 1):

        @pl.when(block >= j)
        def _(j=j):
            for copy in window_copies(j):
                copy.wait_recv()

        @pl.when(block < j)
        def _(j=j):
            place = pl.ds((reach - j) * tokens, tokens)
            kbuf[place, :] = jnp.zeros((tokens, kbuf.shape[1]), BF16)
            vbuf[place, :] = jnp.zeros((tokens, vbuf.shape[1]), BF16)

        @pl.when(block + j < blocks)
        def _(j=j):
            for copy in window_copies(j):
                copy.wait_send()

    attend(block, reach, q_ref, kbuf, vbuf, att_ref)

    for j in range(1, heads):
        ow_copy(others[j - 1], j).wait()
        psend[j - 1] = project(j)
        exchange(j).start()
    ow_copy(head, 0).wait()
    projected = project(0).astype(F32)

    expert_ids = lax.broadcasted_iota(jnp.int32, (count, tokens), 0)
    hits = jnp.zeros((count, tokens), F32)
    for k in range(routes_ref.shape[0]):
        hits = hits + jnp.where(routes_ref[k : k + 1, :] == expert_ids, 1.0, 0.0)
    earlier = jnp.where(
        lax.broadcasted_iota(jnp.int32, (tokens, tokens), 0)
        < lax.broadcasted_iota(jnp.int32, (tokens, tokens), 1),
        1.0,
        0.0,
    ).astype(BF16)
    hits_ref[...] = hits
    before_ref[...] = jnp.dot(hits.astype(BF16), earlier, preferred_element_type=F32)
    residual = res_ref[pl.ds(pl.multiple_of(head * half, 16), half), :].astype(F32)

    for j in range(1, heads):
        exchange(j).wait()
        projected = projected + precv[j - 1].astype(F32)
    hid_ref[...] = (residual + projected).astype(BF16)

    slots = lax.broadcasted_iota(jnp.int32, (cap, tokens), 0).astype(F32)

    def rows_for(expert):
        wanted = hits_ref[pl.ds(expert, 1), :] > 0.5
        picks = jnp.where((slots == before_ref[pl.ds(expert, 1), :]) & wanted, 1.0, 0.0)
        return lax.dot_general(
            picks.astype(BF16),
            hid_ref[...],
            (((1,), (1,)), ((), ())),
            preferred_element_type=F32,
        ).astype(BF16)

    def routed(step):
        turn = turn_of(step, count)
        return pltpu.make_async_remote_copy(
            src_ref=sbuf.at[turn],
            dst_ref=rbuf.at[head, me],
            send_sem=send_sem.at[turn],
            recv_sem=recv_sem.at[me],
            device_id={"ctx": lax.rem(me + turn, count)},
            device_id_type=MESH,
        )

    def landed(source):
        return pltpu.make_async_remote_copy(
            src_ref=rbuf.at[head, source],
            dst_ref=rbuf.at[head, source],
            send_sem=send_sem.at[0],
            recv_sem=recv_sem.at[source],
            device_id={"head": others[0]},
            device_id_type=MESH,
        )

    def crossed(j, source):
        return pltpu.make_async_remote_copy(
            src_ref=rbuf.at[head, source],
            dst_ref=rbuf.at[head, source],
            send_sem=xsend_sem.at[j - 1, source],
            recv_sem=xrecv_sem.at[j - 1, source],
            device_id={"head": others[j - 1]},
            device_id_type=MESH,
        )

    def cross(source):
        for j in range(1, heads):
            crossed(j, source).start()

    def mirror(source):
        for j in range(1, heads):
            origin = lax.rem(head + heads - j, heads)
            pltpu.make_async_remote_copy(
                src_ref=rbuf.at[origin, source],
                dst_ref=rbuf.at[origin, source],
                send_sem=xsend_sem.at[j - 1, source],
                recv_sem=xrecv_sem.at[j - 1, source],
                device_id={"head": others[j - 1]},
                device_id_type=MESH,
            ).wait_recv()

    def dispatch(step, carry):
        turn = turn_of(step, count)
        sbuf[turn] = rows_for(lax.rem(me + turn, count))
        routed(step).start()
        return carry

    lax.fori_loop(0, count - 1, dispatch, 0)
    rbuf[head, me] = rows_for(me)
    cross(me)
    pltpu.make_async_copy(w_hbm, w, w_sem).wait()

    def expert(source):
        squares = jnp.zeros((cap, 1), F32)
        parts = []
        for part in range(heads):
            rows = rbuf[part, source].astype(F32)
            squares = squares + jnp.sum(rows * rows, axis=1, keepdims=True)
            parts.append((rows * gain_ref[part : part + 1, :]).astype(BF16))
        inverse_rms = lax.rsqrt(squares / (heads * half) + 1e-05)

        def product(low):
            total = jnp.zeros((cap, width), F32)
            for part in range(heads):
                total = total + jnp.dot(
                    parts[part],
                    w[part * half : (part + 1) * half, low : low + width],
                    preferred_element_type=F32,
                )
            return total

        gate = product(0) * inverse_rms
        up = product(width) * inverse_rms
        act_ref[source] = (gate * jax.nn.sigmoid(1.702 * gate) * (up + 1.0)).astype(BF16)

    def receive(step, carry):
        source = lax.rem(me + count - turn_of(step, count), count)
        landed(source).wait_recv()
        cross(source)
        before = jnp.where(
            step == 0, me, lax.rem(me + count - turn_of(jnp.maximum(step - 1, 0), count), count)
        )
        mirror(before)
        expert(before)
        return carry

    lax.fori_loop(0, count - 1, receive, 0)
    last = lax.rem(me + count - turn_of(count - 2, count), count)
    mirror(last)
    expert(last)

    def drain(step, carry):
        routed(step).wait_send()
        for j in range(1, heads):
            crossed(j, lax.rem(me + step + 1, count)).wait_send()
        return carry

    lax.fori_loop(0, count - 1, drain, 0)
    for j in range(1, heads):
        crossed(j, me).wait_send()


def body(residual, queries, keys, values, out_weight, norm_gain, routes, expert_weight):
    tokens_here = queries.shape[0]
    heads_count = lax.axis_size("head")
    reach = max(1, lax.axis_size("ctx") // 16) * lax.axis_size("grp")
    width_all = residual.shape[1]
    half = width_all // heads_count
    count = lax.axis_size("ctx")
    experts_all = expert_weight.shape[0] * count
    routed = tokens_here * TOP
    cap = min(tokens_here, routed // experts_all + max(1, routed // (8 * experts_all)))
    hidden_width = expert_weight.shape[3]
    in_vmem = pl.BlockSpec(memory_space=pltpu.VMEM)
    in_hbm = pl.BlockSpec(memory_space=pl.ANY)
    hidden, active = pl.pallas_call(
        functools.partial(layer_kernel, count, cap, reach),
        out_shape=(
            jax.ShapeDtypeStruct((half, tokens_here), BF16),
            jax.ShapeDtypeStruct((count, cap, hidden_width), BF16),
        ),
        in_specs=[in_vmem] * 6 + [in_hbm] * 2,
        out_specs=(in_vmem, in_vmem),
        scratch_shapes=[
            pltpu.VMEM(((reach + 1) * tokens_here, keys.shape[1]), BF16),
            pltpu.VMEM(((reach + 1) * tokens_here, values.shape[1]), BF16),
            pltpu.VMEM(queries.shape, BF16),
            pltpu.VMEM((heads_count, half, out_weight.shape[0]), BF16),
            pltpu.VMEM((width_all, 2 * hidden_width), BF16),
            pltpu.VMEM((heads_count - 1, half, tokens_here), BF16),
            pltpu.VMEM((heads_count - 1, half, tokens_here), BF16),
            pltpu.VMEM((count, tokens_here), F32),
            pltpu.VMEM((count, tokens_here), F32),
            pltpu.VMEM((count, cap, half), BF16),
            pltpu.VMEM((heads_count, count, cap, half), BF16),
            pltpu.SemaphoreType.DMA((2, reach)),
            pltpu.SemaphoreType.DMA((2, reach)),
            pltpu.SemaphoreType.DMA((heads_count,)),
            pltpu.SemaphoreType.DMA,
            pltpu.SemaphoreType.DMA((heads_count - 1,)),
            pltpu.SemaphoreType.DMA((heads_count - 1,)),
            pltpu.SemaphoreType.DMA((count,)),
            pltpu.SemaphoreType.DMA((count,)),
            pltpu.SemaphoreType.DMA((heads_count - 1, count)),
            pltpu.SemaphoreType.DMA((heads_count - 1, count)),
        ],
        compiler_params=pltpu.CompilerParams(
            collective_id=0, has_side_effects=True, vmem_limit_bytes=60 * 1024 * 1024
        ),
    )(
        queries,
        keys,
        values,
        residual.T,
        routes.T,
        norm_gain.reshape(heads_count, half),
        out_weight.T,
        expert_weight[0].reshape(width_all, 2 * hidden_width),
    )
    return (hidden.T, active.reshape(1, 1, count * cap, hidden_width))


def solution(mesh):
    in_specs = (
        P(("ctx", "grp"), None),
        P(("ctx", "grp"), "head"),
        P(("ctx", "grp"), "head"),
        P(("ctx", "grp"), "head"),
        P("head", None),
        P(),
        P(("ctx", "grp"), None),
        P("ctx", None, None, "head"),
    )
    out_specs = (P(("ctx", "grp"), "head"), P("ctx", "grp", None, "head"))
    return jax.shard_map(body, mesh=mesh, in_specs=in_specs, out_specs=out_specs, check_vma=False)
```

```python
import functools
import jax
import jax.numpy as jnp
from jax import lax
from jax.experimental import pallas as pl
from jax.experimental.pallas import tpu as pltpu
from jax.sharding import PartitionSpec as P

D = 2880
HD = 64
TOP = 4


MESH = pl.DeviceIdType.MESH
F32 = jnp.float32
BF16 = jnp.bfloat16


def turn_of(step, count):
    return 1 + lax.rem(step + count // 2 - 1, count - 1)


def in_pair(values, group, lanes):
    zeros = jnp.zeros((values.shape[0], HD), values.dtype)
    if values.shape[1] == HD:
        return jnp.concatenate([values, zeros], 1), jnp.concatenate([zeros, values], 1)
    first = group % 2 == 0
    base = group // 2 * 2 * HD
    pair = values[:, base : base + 2 * HD]
    swapped = jnp.concatenate([pair[:, HD:], pair[:, :HD]], 1)
    low = jnp.where(lanes < HD, pair if first else swapped, jnp.zeros_like(pair))
    high = jnp.where(lanes >= HD, swapped if first else pair, jnp.zeros_like(pair))
    return low, high


def attend(block, reach, q_ref, kbuf, vbuf, att_ref):
    tokens = q_ref.shape[0]
    window = kbuf.shape[0]
    kv_local = kbuf.shape[1] // HD
    pairs = q_ref.shape[1] // (2 * HD * kv_local)
    rows = pairs * tokens
    place = lax.rem(lax.broadcasted_iota(jnp.int32, (rows, window), 0), tokens)
    column = lax.broadcasted_iota(jnp.int32, (rows, window), 1)
    ahead = place + reach * tokens - column
    allowed = (ahead >= 0) & (ahead < reach * tokens) & (column >= (reach - block) * tokens)
    lanes = lax.broadcasted_iota(jnp.int32, (window, 2 * HD), 1)
    left = lax.broadcasted_iota(jnp.int32, (rows, 2 * HD), 1) < HD
    for group in range(kv_local):
        key_pair = in_pair(kbuf[...], group, lanes)
        value_pair = in_pair(vbuf[...], group, lanes)
        first = group * pairs
        queries = jnp.concatenate(
            [
                q_ref[:, (first + p) * 2 * HD : (first + p + 1) * 2 * HD]
                for p in range(pairs)
            ],
            0,
        )
        mixed = jnp.zeros((rows, 2 * HD), F32)
        totals = []
        for side in range(2):
            scores = lax.dot_general(
                queries,
                key_pair[side],
                (((1,), (1,)), ((), ())),
                preferred_element_type=F32,
            )
            scores = jnp.where(allowed, scores * HD ** (-0.5), -1e30)
            row_max = jnp.max(scores, axis=1, keepdims=True)
            weights = jnp.where(allowed, jnp.exp(scores - row_max), 0.0)
            totals.append(jnp.sum(weights, axis=1, keepdims=True))
            mixed = mixed + jnp.dot(
                weights.astype(BF16), value_pair[side], preferred_element_type=F32
            )
        attended = (mixed / jnp.where(left, totals[0], totals[1])).astype(BF16)
        for p in range(pairs):
            att_ref[:, (first + p) * 2 * HD : (first + p + 1) * 2 * HD] = attended[
                p * tokens : (p + 1) * tokens
            ]


def layer_kernel(
    count,
    cap,
    reach,
    q_ref,
    k_ref,
    v_ref,
    res_ref,
    routes_ref,
    gain_ref,
    ow_hbm,
    w_hbm,
    hid_ref,
    act_ref,
    kbuf,
    vbuf,
    att_ref,
    ow,
    paired,
    w,
    psend,
    precv,
    hits_ref,
    before_ref,
    sbuf,
    rbuf,
    ksend_sem,
    krecv_sem,
    ow_sem,
    w_sem,
    psend_sem,
    precv_sem,
    send_sem,
    recv_sem,
    xsend_sem,
    xrecv_sem,
):
    me = lax.axis_index("ctx")
    head = lax.axis_index("head")
    heads = rbuf.shape[0]
    others = [lax.rem(head + j, heads) for j in range(1, heads)]
    half, tokens = hid_ref.shape
    width = act_ref.shape[2]

    def ow_copy(which, slot):
        rows = pl.ds(pl.multiple_of(which * half, 16), half)
        return pltpu.make_async_copy(ow_hbm.at[rows], ow.at[slot], ow_sem.at[slot])

    for j in range(1, heads):
        ow_copy(others[j - 1], j).start()
    ow_copy(head, 0).start()
    pltpu.make_async_copy(w_hbm, paired, w_sem).start()

    barrier = pltpu.get_barrier_semaphore()
    for other in others:
        pl.semaphore_signal(barrier, inc=1, device_id={"head": other}, device_id_type=MESH)

    def greet(step, carry):
        peer = lax.rem(me + step, count)
        pl.semaphore_signal(barrier, inc=1, device_id={"ctx": peer}, device_id_type=MESH)
        return carry

    lax.fori_loop(1, count, greet, 0)

    groups = lax.axis_size("grp")
    block = me * groups + lax.axis_index("grp")
    blocks = count * groups

    def at_block(index):
        return {"ctx": index // groups, "grp": lax.rem(index, groups)}

    for j in range(1, reach + 1):
        for peer in (lax.rem(block + j, blocks), lax.rem(block + blocks - j, blocks)):
            pl.semaphore_signal(barrier, inc=1, device_id=at_block(peer), device_id_type=MESH)

    def window_copies(j):
        place = pl.ds((reach - j) * tokens, tokens)
        target = at_block(lax.rem(block + j, blocks))
        return [
            pltpu.make_async_remote_copy(
                src_ref=source,
                dst_ref=buffer.at[place],
                send_sem=ksend_sem.at[n, j - 1],
                recv_sem=krecv_sem.at[n, j - 1],
                device_id=target,
                device_id_type=MESH,
            )
            for n, (source, buffer) in enumerate(((k_ref, kbuf), (v_ref, vbuf)))
        ]

    pl.semaphore_wait(barrier, count - 1 + heads - 1 + 2 * reach)
    for j in range(1, reach + 1):

        @pl.when(block + j < blocks)
        def _(j=j):
            for copy in window_copies(j):
                copy.start()

    kbuf[reach * tokens :, :] = k_ref[...]
    vbuf[reach * tokens :, :] = v_ref[...]

    def project(slot):
        return lax.dot_general(
            ow[slot], att_ref[...], (((1,), (1,)), ((), ())), preferred_element_type=F32
        ).astype(BF16)

    def exchange(j):
        return pltpu.make_async_remote_copy(
            src_ref=psend.at[j - 1],
            dst_ref=precv.at[j - 1],
            send_sem=psend_sem.at[j - 1],
            recv_sem=precv_sem.at[j - 1],
            device_id={"head": others[j - 1]},
            device_id_type=MESH,
        )

    for j in range(1, reach + 1):

        @pl.when(block >= j)
        def _(j=j):
            for copy in window_copies(j):
                copy.wait_recv()

        @pl.when(block < j)
        def _(j=j):
            place = pl.ds((reach - j) * tokens, tokens)
            kbuf[place, :] = jnp.zeros((tokens, kbuf.shape[1]), BF16)
            vbuf[place, :] = jnp.zeros((tokens, vbuf.shape[1]), BF16)

        @pl.when(block + j < blocks)
        def _(j=j):
            for copy in window_copies(j):
                copy.wait_send()

    attend(block, reach, q_ref, kbuf, vbuf, att_ref)

    for j in range(1, heads):
        ow_copy(others[j - 1], j).wait()
        psend[j - 1] = project(j)
        exchange(j).start()
    ow_copy(head, 0).wait()
    projected = project(0).astype(F32)

    expert_ids = lax.broadcasted_iota(jnp.int32, (count, tokens), 0)
    hits = jnp.zeros((count, tokens), F32)
    for k in range(routes_ref.shape[0]):
        hits = hits + jnp.where(routes_ref[k : k + 1, :] == expert_ids, 1.0, 0.0)
    earlier = jnp.where(
        lax.broadcasted_iota(jnp.int32, (tokens, tokens), 0)
        < lax.broadcasted_iota(jnp.int32, (tokens, tokens), 1),
        1.0,
        0.0,
    ).astype(BF16)
    hits_ref[...] = hits
    before_ref[...] = jnp.dot(hits.astype(BF16), earlier, preferred_element_type=F32)
    residual = res_ref[pl.ds(pl.multiple_of(head * half, 16), half), :].astype(F32)

    for j in range(1, heads):
        exchange(j).wait()
        projected = projected + precv[j - 1].astype(F32)
    hid_ref[...] = (residual + projected).astype(BF16)

    slots = lax.broadcasted_iota(jnp.int32, (cap, tokens), 0).astype(F32)

    def rows_for(expert):
        wanted = hits_ref[pl.ds(expert, 1), :] > 0.5
        picks = jnp.where((slots == before_ref[pl.ds(expert, 1), :]) & wanted, 1.0, 0.0)
        return lax.dot_general(
            picks.astype(BF16),
            hid_ref[...],
            (((1,), (1,)), ((), ())),
            preferred_element_type=F32,
        ).astype(BF16)

    def routed(step):
        turn = turn_of(step, count)
        return pltpu.make_async_remote_copy(
            src_ref=sbuf.at[turn],
            dst_ref=rbuf.at[head, me],
            send_sem=send_sem.at[turn],
            recv_sem=recv_sem.at[me],
            device_id={"ctx": lax.rem(me + turn, count)},
            device_id_type=MESH,
        )

    def landed(source):
        return pltpu.make_async_remote_copy(
            src_ref=rbuf.at[head, source],
            dst_ref=rbuf.at[head, source],
            send_sem=send_sem.at[0],
            recv_sem=recv_sem.at[source],
            device_id={"head": others[0]},
            device_id_type=MESH,
        )

    def crossed(j, source):
        return pltpu.make_async_remote_copy(
            src_ref=rbuf.at[head, source],
            dst_ref=rbuf.at[head, source],
            send_sem=xsend_sem.at[j - 1, source],
            recv_sem=xrecv_sem.at[j - 1, source],
            device_id={"head": others[j - 1]},
            device_id_type=MESH,
        )

    def cross(source):
        for j in range(1, heads):
            crossed(j, source).start()

    def mirror(source):
        for j in range(1, heads):
            origin = lax.rem(head + heads - j, heads)
            pltpu.make_async_remote_copy(
                src_ref=rbuf.at[origin, source],
                dst_ref=rbuf.at[origin, source],
                send_sem=xsend_sem.at[j - 1, source],
                recv_sem=xrecv_sem.at[j - 1, source],
                device_id={"head": others[j - 1]},
                device_id_type=MESH,
            ).wait_recv()

    def dispatch(step, carry):
        turn = turn_of(step, count)
        sbuf[turn] = rows_for(lax.rem(me + turn, count))
        routed(step).start()
        return carry

    lax.fori_loop(0, count - 1, dispatch, 0)
    rbuf[head, me] = rows_for(me)
    cross(me)
    pltpu.make_async_copy(w_hbm, paired, w_sem).wait()

    def unpair(step, carry):
        rows = pl.ds(pl.multiple_of(step * 32, 32), 32)
        pair = paired[rows]
        w[rows, :width] = pair[:, 0, :]
        w[rows, width:] = pair[:, 1, :]
        return carry

    lax.fori_loop(0, w.shape[0] // 32, unpair, 0)

    def expert(source):
        squares = jnp.zeros((cap, 1), F32)
        parts = []
        for part in range(heads):
            rows = rbuf[part, source].astype(F32)
            squares = squares + jnp.sum(rows * rows, axis=1, keepdims=True)
            parts.append((rows * gain_ref[part : part + 1, :]).astype(BF16))
        inverse_rms = lax.rsqrt(squares / (heads * half) + 1e-05)

        def product(low):
            total = jnp.zeros((cap, width), F32)
            for part in range(heads):
                total = total + jnp.dot(
                    parts[part],
                    w[part * half : (part + 1) * half, low : low + width],
                    preferred_element_type=F32,
                )
            return total

        gate = product(0) * inverse_rms
        up = product(width) * inverse_rms
        act_ref[source] = (gate * jax.nn.sigmoid(1.702 * gate) * (up + 1.0)).astype(BF16)

    def receive(step, carry):
        source = lax.rem(me + count - turn_of(step, count), count)
        landed(source).wait_recv()
        cross(source)
        before = jnp.where(
            step == 0, me, lax.rem(me + count - turn_of(jnp.maximum(step - 1, 0), count), count)
        )
        mirror(before)
        expert(before)
        return carry

    lax.fori_loop(0, count - 1, receive, 0)
    last = lax.rem(me + count - turn_of(count - 2, count), count)
    mirror(last)
    expert(last)

    def drain(step, carry):
        routed(step).wait_send()
        for j in range(1, heads):
            crossed(j, lax.rem(me + step + 1, count)).wait_send()
        return carry

    lax.fori_loop(0, count - 1, drain, 0)
    for j in range(1, heads):
        crossed(j, me).wait_send()


def body(residual, queries, keys, values, out_weight, norm_gain, routes, expert_weight):
    tokens_here = queries.shape[0]
    heads_count = lax.axis_size("head")
    reach = max(1, lax.axis_size("ctx") // 16) * lax.axis_size("grp")
    width_all = residual.shape[1]
    half = width_all // heads_count
    count = lax.axis_size("ctx")
    experts_all = expert_weight.shape[0] * count
    routed = tokens_here * TOP
    cap = min(tokens_here, routed // experts_all + max(1, routed // (8 * experts_all)))
    hidden_width = expert_weight.shape[3]
    in_vmem = pl.BlockSpec(memory_space=pltpu.VMEM)
    in_hbm = pl.BlockSpec(memory_space=pl.ANY)
    hidden, active = pl.pallas_call(
        functools.partial(layer_kernel, count, cap, reach),
        out_shape=(
            jax.ShapeDtypeStruct((half, tokens_here), BF16),
            jax.ShapeDtypeStruct((count, cap, hidden_width), BF16),
        ),
        in_specs=[in_vmem] * 6 + [in_hbm] * 2,
        out_specs=(in_vmem, in_vmem),
        scratch_shapes=[
            pltpu.VMEM(((reach + 1) * tokens_here, keys.shape[1]), BF16),
            pltpu.VMEM(((reach + 1) * tokens_here, values.shape[1]), BF16),
            pltpu.VMEM(queries.shape, BF16),
            pltpu.VMEM((heads_count, half, out_weight.shape[0]), BF16),
            pltpu.VMEM((width_all, 2, hidden_width), BF16),
            pltpu.VMEM((width_all, 2 * hidden_width), BF16),
            pltpu.VMEM((heads_count - 1, half, tokens_here), BF16),
            pltpu.VMEM((heads_count - 1, half, tokens_here), BF16),
            pltpu.VMEM((count, tokens_here), F32),
            pltpu.VMEM((count, tokens_here), F32),
            pltpu.VMEM((count, cap, half), BF16),
            pltpu.VMEM((heads_count, count, cap, half), BF16),
            pltpu.SemaphoreType.DMA((2, reach)),
            pltpu.SemaphoreType.DMA((2, reach)),
            pltpu.SemaphoreType.DMA((heads_count,)),
            pltpu.SemaphoreType.DMA,
            pltpu.SemaphoreType.DMA((heads_count - 1,)),
            pltpu.SemaphoreType.DMA((heads_count - 1,)),
            pltpu.SemaphoreType.DMA((count,)),
            pltpu.SemaphoreType.DMA((count,)),
            pltpu.SemaphoreType.DMA((heads_count - 1, count)),
            pltpu.SemaphoreType.DMA((heads_count - 1, count)),
        ],
        compiler_params=pltpu.CompilerParams(
            collective_id=0, has_side_effects=True, vmem_limit_bytes=60 * 1024 * 1024
        ),
    )(
        queries,
        keys,
        values,
        residual.T,
        routes.T,
        norm_gain.reshape(heads_count, half),
        out_weight.T,
        expert_weight[0],
    )
    return (hidden.T, active.reshape(1, 1, count * cap, hidden_width))


def solution(mesh):
    in_specs = (
        P(("ctx", "grp"), None),
        P(("ctx", "grp"), "head"),
        P(("ctx", "grp"), "head"),
        P(("ctx", "grp"), "head"),
        P("head", None),
        P(),
        P(("ctx", "grp"), None),
        P("ctx", None, None, "head"),
    )
    out_specs = (P(("ctx", "grp"), "head"), P("ctx", "grp", None, "head"))
    return jax.shard_map(body, mesh=mesh, in_specs=in_specs, out_specs=out_specs, check_vma=False)
```

```python
import functools
import jax
import jax.numpy as jnp
from jax import lax
from jax.experimental import pallas as pl
from jax.experimental.pallas import tpu as pltpu
from jax.sharding import PartitionSpec as P

D = 2880
HD = 64
TOP = 4


MESH = pl.DeviceIdType.MESH
F32 = jnp.float32
BF16 = jnp.bfloat16


def turn_of(step, count):
    return 1 + lax.rem(step + count // 2 - 1, count - 1)


def in_pair(values, group, lanes):
    zeros = jnp.zeros((values.shape[0], HD), values.dtype)
    if values.shape[1] == HD:
        return jnp.concatenate([values, zeros], 1), jnp.concatenate([zeros, values], 1)
    first = group % 2 == 0
    base = group // 2 * 2 * HD
    pair = values[:, base : base + 2 * HD]
    swapped = jnp.concatenate([pair[:, HD:], pair[:, :HD]], 1)
    low = jnp.where(lanes < HD, pair if first else swapped, jnp.zeros_like(pair))
    high = jnp.where(lanes >= HD, swapped if first else pair, jnp.zeros_like(pair))
    return low, high


def attend(block, reach, q_ref, kbuf, vbuf, att_ref):
    tokens = q_ref.shape[0]
    window = kbuf.shape[0]
    kv_local = kbuf.shape[1] // HD
    pairs = q_ref.shape[1] // (2 * HD * kv_local)
    rows = pairs * tokens
    place = lax.rem(lax.broadcasted_iota(jnp.int32, (rows, window), 0), tokens)
    column = lax.broadcasted_iota(jnp.int32, (rows, window), 1)
    ahead = place + reach * tokens - column
    allowed = (ahead >= 0) & (ahead < reach * tokens) & (column >= (reach - block) * tokens)
    lanes = lax.broadcasted_iota(jnp.int32, (window, 2 * HD), 1)
    left = lax.broadcasted_iota(jnp.int32, (rows, 2 * HD), 1) < HD
    for group in range(kv_local):
        key_pair = in_pair(kbuf[...], group, lanes)
        value_pair = in_pair(vbuf[...], group, lanes)
        first = group * pairs
        queries = jnp.concatenate(
            [
                q_ref[:, (first + p) * 2 * HD : (first + p + 1) * 2 * HD]
                for p in range(pairs)
            ],
            0,
        )
        mixed = jnp.zeros((rows, 2 * HD), F32)
        totals = []
        for side in range(2):
            scores = lax.dot_general(
                queries,
                key_pair[side],
                (((1,), (1,)), ((), ())),
                preferred_element_type=F32,
            )
            scores = jnp.where(allowed, scores * HD ** (-0.5), -1e30)
            row_max = jnp.max(scores, axis=1, keepdims=True)
            weights = jnp.where(allowed, jnp.exp(scores - row_max), 0.0)
            totals.append(jnp.sum(weights, axis=1, keepdims=True))
            mixed = mixed + jnp.dot(
                weights.astype(BF16), value_pair[side], preferred_element_type=F32
            )
        attended = (mixed / jnp.where(left, totals[0], totals[1])).astype(BF16)
        for p in range(pairs):
            att_ref[:, (first + p) * 2 * HD : (first + p + 1) * 2 * HD] = attended[
                p * tokens : (p + 1) * tokens
            ]


def layer_kernel(
    count,
    cap,
    reach,
    q_ref,
    k_ref,
    v_ref,
    res_ref,
    routes_ref,
    gain_ref,
    ow_hbm,
    w_hbm,
    hid_ref,
    act_ref,
    kbuf,
    vbuf,
    att_ref,
    ow,
    paired,
    w,
    psend,
    precv,
    hits_ref,
    before_ref,
    sbuf,
    rbuf,
    ksend_sem,
    krecv_sem,
    ow_sem,
    w_sem,
    psend_sem,
    precv_sem,
    send_sem,
    recv_sem,
    xsend_sem,
    xrecv_sem,
):
    me = lax.axis_index("ctx")
    head = lax.axis_index("head")
    heads = rbuf.shape[0]
    others = [lax.rem(head + j, heads) for j in range(1, heads)]
    half, tokens = hid_ref.shape
    width = act_ref.shape[2]

    def ow_copy(which, slot):
        rows = pl.ds(pl.multiple_of(which * half, 16), half)
        return pltpu.make_async_copy(ow_hbm.at[rows], ow.at[slot], ow_sem.at[slot])

    for j in range(1, heads):
        ow_copy(others[j - 1], j).start()
    ow_copy(head, 0).start()
    pltpu.make_async_copy(w_hbm, paired, w_sem).start()

    barrier = pltpu.get_barrier_semaphore()
    for other in others:
        pl.semaphore_signal(barrier, inc=1, device_id={"head": other}, device_id_type=MESH)

    def greet(step, carry):
        peer = lax.rem(me + step, count)
        pl.semaphore_signal(barrier, inc=1, device_id={"ctx": peer}, device_id_type=MESH)
        return carry

    lax.fori_loop(1, count, greet, 0)

    groups = lax.axis_size("grp")
    block = me * groups + lax.axis_index("grp")
    blocks = count * groups

    def at_block(index):
        return {"ctx": index // groups, "grp": lax.rem(index, groups)}

    for j in range(1, reach + 1):
        for peer in (lax.rem(block + j, blocks), lax.rem(block + blocks - j, blocks)):
            pl.semaphore_signal(barrier, inc=1, device_id=at_block(peer), device_id_type=MESH)

    def window_copies(j):
        place = pl.ds((reach - j) * tokens, tokens)
        target = at_block(lax.rem(block + j, blocks))
        return [
            pltpu.make_async_remote_copy(
                src_ref=source,
                dst_ref=buffer.at[place],
                send_sem=ksend_sem.at[n, j - 1],
                recv_sem=krecv_sem.at[n, j - 1],
                device_id=target,
                device_id_type=MESH,
            )
            for n, (source, buffer) in enumerate(((k_ref, kbuf), (v_ref, vbuf)))
        ]

    pl.semaphore_wait(barrier, count - 1 + heads - 1 + 2 * reach)
    for j in range(1, reach + 1):

        @pl.when(block + j < blocks)
        def _(j=j):
            for copy in window_copies(j):
                copy.start()

    kbuf[reach * tokens :, :] = k_ref[...]
    vbuf[reach * tokens :, :] = v_ref[...]

    def project(slot):
        return lax.dot_general(
            ow[slot], att_ref[...], (((1,), (1,)), ((), ())), preferred_element_type=F32
        ).astype(BF16)

    def exchange(j):
        return pltpu.make_async_remote_copy(
            src_ref=psend.at[j - 1],
            dst_ref=precv.at[j - 1],
            send_sem=psend_sem.at[j - 1],
            recv_sem=precv_sem.at[j - 1],
            device_id={"head": others[j - 1]},
            device_id_type=MESH,
        )

    for j in range(1, reach + 1):

        @pl.when(block >= j)
        def _(j=j):
            for copy in window_copies(j):
                copy.wait_recv()

        @pl.when(block < j)
        def _(j=j):
            place = pl.ds((reach - j) * tokens, tokens)
            kbuf[place, :] = jnp.zeros((tokens, kbuf.shape[1]), BF16)
            vbuf[place, :] = jnp.zeros((tokens, vbuf.shape[1]), BF16)

        @pl.when(block + j < blocks)
        def _(j=j):
            for copy in window_copies(j):
                copy.wait_send()

    attend(block, reach, q_ref, kbuf, vbuf, att_ref)

    for j in range(1, heads):
        ow_copy(others[j - 1], j).wait()
        psend[j - 1] = project(j)
        exchange(j).start()
    ow_copy(head, 0).wait()
    projected = project(0).astype(F32)

    expert_ids = lax.broadcasted_iota(jnp.int32, (count, tokens), 0)
    hits = jnp.zeros((count, tokens), F32)
    for k in range(routes_ref.shape[0]):
        hits = hits + jnp.where(routes_ref[k : k + 1, :] == expert_ids, 1.0, 0.0)
    earlier = jnp.where(
        lax.broadcasted_iota(jnp.int32, (tokens, tokens), 0)
        < lax.broadcasted_iota(jnp.int32, (tokens, tokens), 1),
        1.0,
        0.0,
    ).astype(BF16)
    hits_ref[...] = hits
    before_ref[...] = jnp.dot(hits.astype(BF16), earlier, preferred_element_type=F32)
    residual = res_ref[pl.ds(pl.multiple_of(head * half, 16), half), :].astype(F32)

    for j in range(1, heads):
        exchange(j).wait()
        projected = projected + precv[j - 1].astype(F32)
    hid_ref[...] = (residual + projected).astype(BF16)

    slots = lax.broadcasted_iota(jnp.int32, (cap, tokens), 0).astype(F32)

    def rows_for(expert):
        wanted = hits_ref[pl.ds(expert, 1), :] > 0.5
        picks = jnp.where((slots == before_ref[pl.ds(expert, 1), :]) & wanted, 1.0, 0.0)
        return lax.dot_general(
            picks.astype(BF16),
            hid_ref[...],
            (((1,), (1,)), ((), ())),
            preferred_element_type=F32,
        ).astype(BF16)

    def routed(step):
        turn = turn_of(step, count)
        return pltpu.make_async_remote_copy(
            src_ref=sbuf.at[turn],
            dst_ref=rbuf.at[head, me],
            send_sem=send_sem.at[turn],
            recv_sem=recv_sem.at[me],
            device_id={"ctx": lax.rem(me + turn, count)},
            device_id_type=MESH,
        )

    def landed(source):
        return pltpu.make_async_remote_copy(
            src_ref=rbuf.at[head, source],
            dst_ref=rbuf.at[head, source],
            send_sem=send_sem.at[0],
            recv_sem=recv_sem.at[source],
            device_id={"head": others[0]},
            device_id_type=MESH,
        )

    def crossed(j, source):
        return pltpu.make_async_remote_copy(
            src_ref=rbuf.at[head, source],
            dst_ref=rbuf.at[head, source],
            send_sem=xsend_sem.at[j - 1, source],
            recv_sem=xrecv_sem.at[j - 1, source],
            device_id={"head": others[j - 1]},
            device_id_type=MESH,
        )

    def cross(source):
        for j in range(1, heads):
            crossed(j, source).start()

    def mirror(source):
        for j in range(1, heads):
            origin = lax.rem(head + heads - j, heads)
            pltpu.make_async_remote_copy(
                src_ref=rbuf.at[origin, source],
                dst_ref=rbuf.at[origin, source],
                send_sem=xsend_sem.at[j - 1, source],
                recv_sem=xrecv_sem.at[j - 1, source],
                device_id={"head": others[j - 1]},
                device_id_type=MESH,
            ).wait_recv()

    def dispatch(step, carry):
        turn = turn_of(step, count)
        sbuf[turn] = rows_for(lax.rem(me + turn, count))
        routed(step).start()
        return carry

    lax.fori_loop(0, count - 1, dispatch, 0)
    rbuf[head, me] = rows_for(me)
    cross(me)
    pltpu.make_async_copy(w_hbm, paired, w_sem).wait()

    def unpair(step, carry):
        rows = pl.ds(pl.multiple_of(step * 32, 32), 32)
        pair = paired[rows]
        w[rows, :width] = pair[:, 0, :]
        w[rows, width:] = pair[:, 1, :]
        return carry

    pieces = w.shape[0] // 32
    early = count // 2 - 1

    def expert(source):
        squares = jnp.zeros((cap, 1), F32)
        parts = []
        for part in range(heads):
            rows = rbuf[part, source].astype(F32)
            squares = squares + jnp.sum(rows * rows, axis=1, keepdims=True)
            parts.append((rows * gain_ref[part : part + 1, :]).astype(BF16))
        inverse_rms = lax.rsqrt(squares / (heads * half) + 1e-05)

        def product(low):
            total = jnp.zeros((cap, width), F32)
            for part in range(heads):
                total = total + jnp.dot(
                    parts[part],
                    w[part * half : (part + 1) * half, low : low + width],
                    preferred_element_type=F32,
                )
            return total

        gate = product(0) * inverse_rms
        up = product(width) * inverse_rms
        act_ref[source] = (gate * jax.nn.sigmoid(1.702 * gate) * (up + 1.0)).astype(BF16)

    def source_at(place):
        turn = turn_of(jnp.maximum(place - 1, 0), count)
        return jnp.where(place == 0, me, lax.rem(me + count - turn, count))

    def forward(step):
        source = lax.rem(me + count - turn_of(step, count), count)
        landed(source).wait_recv()
        cross(source)

    def receive_early(step, carry):
        lax.fori_loop(step * pieces // early, (step + 1) * pieces // early, unpair, 0)
        forward(step)
        return carry

    def receive(step, carry):
        forward(step)
        for side in range(2):
            source = source_at(2 * (step - early) + side)
            mirror(source)
            expert(source)
        return carry

    lax.fori_loop(0, early, receive_early, 0)
    lax.fori_loop(early, count - 1, receive, 0)

    def drain(step, carry):
        routed(step).wait_send()
        for j in range(1, heads):
            crossed(j, lax.rem(me + step + 1, count)).wait_send()
        return carry

    lax.fori_loop(0, count - 1, drain, 0)
    for j in range(1, heads):
        crossed(j, me).wait_send()


def body(residual, queries, keys, values, out_weight, norm_gain, routes, expert_weight):
    tokens_here = queries.shape[0]
    heads_count = lax.axis_size("head")
    reach = max(1, lax.axis_size("ctx") // 16) * lax.axis_size("grp")
    width_all = residual.shape[1]
    half = width_all // heads_count
    count = lax.axis_size("ctx")
    experts_all = expert_weight.shape[0] * count
    routed = tokens_here * TOP
    cap = min(tokens_here, routed // experts_all + max(1, routed // (8 * experts_all)))
    hidden_width = expert_weight.shape[3]
    in_vmem = pl.BlockSpec(memory_space=pltpu.VMEM)
    in_hbm = pl.BlockSpec(memory_space=pl.ANY)
    hidden, active = pl.pallas_call(
        functools.partial(layer_kernel, count, cap, reach),
        out_shape=(
            jax.ShapeDtypeStruct((half, tokens_here), BF16),
            jax.ShapeDtypeStruct((count, cap, hidden_width), BF16),
        ),
        in_specs=[in_vmem] * 6 + [in_hbm] * 2,
        out_specs=(in_vmem, in_vmem),
        scratch_shapes=[
            pltpu.VMEM(((reach + 1) * tokens_here, keys.shape[1]), BF16),
            pltpu.VMEM(((reach + 1) * tokens_here, values.shape[1]), BF16),
            pltpu.VMEM(queries.shape, BF16),
            pltpu.VMEM((heads_count, half, out_weight.shape[0]), BF16),
            pltpu.VMEM((width_all, 2, hidden_width), BF16),
            pltpu.VMEM((width_all, 2 * hidden_width), BF16),
            pltpu.VMEM((heads_count - 1, half, tokens_here), BF16),
            pltpu.VMEM((heads_count - 1, half, tokens_here), BF16),
            pltpu.VMEM((count, tokens_here), F32),
            pltpu.VMEM((count, tokens_here), F32),
            pltpu.VMEM((count, cap, half), BF16),
            pltpu.VMEM((heads_count, count, cap, half), BF16),
            pltpu.SemaphoreType.DMA((2, reach)),
            pltpu.SemaphoreType.DMA((2, reach)),
            pltpu.SemaphoreType.DMA((heads_count,)),
            pltpu.SemaphoreType.DMA,
            pltpu.SemaphoreType.DMA((heads_count - 1,)),
            pltpu.SemaphoreType.DMA((heads_count - 1,)),
            pltpu.SemaphoreType.DMA((count,)),
            pltpu.SemaphoreType.DMA((count,)),
            pltpu.SemaphoreType.DMA((heads_count - 1, count)),
            pltpu.SemaphoreType.DMA((heads_count - 1, count)),
        ],
        compiler_params=pltpu.CompilerParams(
            collective_id=0, has_side_effects=True, vmem_limit_bytes=60 * 1024 * 1024
        ),
    )(
        queries,
        keys,
        values,
        residual.T,
        routes.T,
        norm_gain.reshape(heads_count, half),
        out_weight.T,
        expert_weight[0],
    )
    return (hidden.T, active.reshape(1, 1, count * cap, hidden_width))


def solution(mesh):
    in_specs = (
        P(("ctx", "grp"), None),
        P(("ctx", "grp"), "head"),
        P(("ctx", "grp"), "head"),
        P(("ctx", "grp"), "head"),
        P("head", None),
        P(),
        P(("ctx", "grp"), None),
        P("ctx", None, None, "head"),
    )
    out_specs = (P(("ctx", "grp"), "head"), P("ctx", "grp", None, "head"))
    return jax.shard_map(body, mesh=mesh, in_specs=in_specs, out_specs=out_specs, check_vma=False)
```
